32 devices in a mesh: fsdp: 32 (over z, y, x, core).
Axes of the slice: x: 2, y: 2, z: 4, core: 2. Of those that a mesh axis runs over, the one named last changes fastest.
Arguments:
- tokens: bfloat16 [32, 512, 1024], P('fsdp'), may hold values from -6 to 6
- cotangent: bfloat16 [32, 512, 1024], P('fsdp'), may hold values from -6 to 6
- segments: int32 [32, 512], P('fsdp'), may hold values from 0 to 25, as said below
- adapter_id: int32 [32], P('fsdp'), may hold values from 0 to 7
- input_weight: bfloat16 [3, 1024, 1024], P(None, 'fsdp'), may hold values from -0.1875 to 0.1875
- output_weight: bfloat16 [1024, 1024], P('fsdp'), may hold values from -0.75 to 0.75
- norm_gain: bfloat16 [2, 1024], P(None, 'fsdp'), may hold values from 0.5 to 1.5
- norm_shift: bfloat16 [2, 1024], P(None, 'fsdp'), may hold values from -1.75 to 1.75
- attention_down: bfloat16 [4, 8, 1024, 16], P(None, None, 'fsdp'), may hold values from -0.1875 to 0.1875
- attention_up: bfloat16 [4, 8, 16, 1024], P(None, None, None, 'fsdp'), may hold values from -0.75 to 0.75
- expand_weight: bfloat16 [1024, 4096], P('fsdp'), may hold values from -0.1875 to 0.1875
- reduce_weight: bfloat16 [4096, 1024], P('fsdp'), may hold values from -0.09375 to 0.09375
- expand_down: bfloat16 [8, 1024, 16], P(None, 'fsdp'), may hold values from -0.1875 to 0.1875
- expand_up: bfloat16 [8, 16, 4096], P(None, None, 'fsdp'), may hold values from -0.75 to 0.75
- reduce_down: bfloat16 [8, 4096, 16], P(None, 'fsdp'), may hold values from -0.09375 to 0.09375
- reduce_up: bfloat16 [8, 16, 1024], P(None, None, 'fsdp'), may hold values from -0.75 to 0.75
Outputs:
- layer_output: bfloat16 [32, 512, 1024], P('fsdp')
- input_gradient: float32 [32, 512, 1024], P('fsdp')
- attention_down_gradient: float32 [4, 8, 1024, 16], P(None, None, 'fsdp')
- attention_up_gradient: float32 [4, 8, 16, 1024], P(None, None, None, 'fsdp')
- expand_down_gradient: float32 [8, 1024, 16], P(None, 'fsdp')
- expand_up_gradient: float32 [8, 16, 4096], P(None, None, 'fsdp')
- reduce_down_gradient: float32 [8, 4096, 16], P(None, 'fsdp')
- reduce_up_gradient: float32 [8, 16, 1024], P(None, None, 'fsdp')
The draws below stay inside these ranges and needn't reach their ends.
Inputs may be any that keep to these rules, and one draw needn't show every extreme that they name: `segments`: in each sequence the numbers start at 0 at the first token and rise by one at each document's first token; every document but a sequence's last has 20 to 200 tokens; in one sequence of every draw every document but the last has exactly 20 tokens.
All inputs are finite; a program needn't handle non-finite values.
Results may differ from the reference program's by a relative error of at most 0.015.
Values may be sent and summed in bfloat16 or wider, within the bound.
No kernel may reach another device: no remote copies, remote signals or barrier semaphores. Data moves between devices by JAX's collectives and lax.ppermute only.
A program may use at most 192 MiB of HBM per device.

```python
import math
import jax
import jax.numpy as jnp
from jax import lax

D = 1024
FF = 4096
HEADS = 16
HEAD_DIM = 64
RANK = 16
ADAPT = 8
SEQ_LEN = 512
DOC_MIN = 20
DOC_MAX = 200
SEQS = 32


def draw_segments(key, part):
    doc_key = jax.random.fold_in(key, 17)
    most_docs = SEQ_LEN // DOC_MIN + 1
    doc_lengths = jax.random.randint(doc_key, (SEQS, most_docs), DOC_MIN, DOC_MAX + 1, dtype=jnp.int32)
    first_row = (jnp.arange(SEQS, dtype=jnp.int32) == 0)[:, None]
    doc_lengths = jnp.where(first_row, jnp.int32(DOC_MIN), doc_lengths).astype(jnp.int32)
    doc_ends = jnp.cumsum(doc_lengths, axis=1).astype(jnp.int32)
    places = jnp.arange(SEQ_LEN, dtype=jnp.int32)
    passed = (doc_ends[:, None, :] <= places[None, :, None]).astype(jnp.int32)
    return jnp.sum(passed, axis=-1).astype(jnp.int32)


def set_ends(drawn, rng, least, largest):
    spot = [jax.random.randint(jax.random.fold_in(rng, axis), (), 0, length) for axis, length in enumerate(drawn.shape)]
    longest = drawn.shape.index(max(drawn.shape))
    next_to = spot[:longest] + [(spot[longest] + 1) % drawn.shape[longest]] + spot[longest + 1:]
    return drawn.at[tuple(spot)].set(least).at[tuple(next_to)].set(largest)


def level_of(key, dims, split, low, largest):
    gain = 1.0
    for position, shards_of in split:
        heights = jax.random.uniform(jax.random.fold_in(jax.random.fold_in(key, 6), position), (shards_of,), jnp.float32, low / len(split), largest / len(split))
        gain = gain * jnp.repeat(jnp.exp(heights), dims[position] // shards_of).reshape((-1,) + (1,) * (len(dims) - 1 - position))
    return gain


def noise(key, shape, width, reach, cuts=(), held_as=jnp.bfloat16):
    drawn = jax.random.normal(key, shape, jnp.float32) * width
    if len(cuts) > 0:
        drawn = level_of(key, shape, cuts, -0.22, 0.18) * drawn
    return jnp.clip(drawn, min=-reach, max=reach).astype(held_as)


def setup_inputs(seed: int = 0) -> dict:
    streams_of = jax.random.split(jax.random.key(seed), 17)
    tokens = noise(streams_of[0], (SEQS, SEQ_LEN, D), 1.0, 6.0, ((0, 32),))
    cotangent = noise(streams_of[1], (SEQS, SEQ_LEN, D), 1.0, 6.0, ((0, 32),))
    segments = draw_segments(jax.random.fold_in(streams_of[16], 71), 0)
    adapter_id = set_ends(jax.random.randint(streams_of[3], (SEQS,), 0, ADAPT), jax.random.fold_in(streams_of[3], 1), 0, ADAPT - 1).astype(jnp.int32)
    input_weight = noise(streams_of[4], (3, D, D), D ** -0.5, 0.1875, ((1, 32),))
    output_weight = noise(streams_of[5], (D, D), (D // 16) ** -0.5, 0.75, ((0, 32),))
    norm_gain = jnp.clip(1.0 + 0.1 * jax.random.normal(streams_of[6], (2, D), jnp.float32), 0.5, 1.5).astype(jnp.bfloat16)
    norm_shift = noise(streams_of[7], (2, D), 0.3, 1.75, ((1, 32),))
    attention_down = noise(streams_of[8], (4, ADAPT, D, RANK), D ** -0.5, 0.1875, ((2, 32),))
    attention_up = noise(streams_of[9], (4, ADAPT, RANK, D), (4 * RANK) ** -0.5, 0.75, ((3, 32),))
    expand_weight = noise(streams_of[10], (D, FF), D ** -0.5, 0.1875, ((0, 32),))
    reduce_weight = noise(streams_of[11], (FF, D), FF ** -0.5, 0.09375, ((0, 32),))
    expand_down = noise(streams_of[12], (ADAPT, D, RANK), D ** -0.5, 0.1875, ((1, 32),))
    expand_up = noise(streams_of[13], (ADAPT, RANK, FF), (4 * RANK) ** -0.5, 0.75, ((2, 32),))
    reduce_down = noise(streams_of[14], (ADAPT, FF, RANK), FF ** -0.5, 0.09375, ((1, 32),))
    reduce_up = noise(streams_of[15], (ADAPT, RANK, D), (4 * RANK) ** -0.5, 0.75, ((2, 32),))
    return {"tokens": tokens, "cotangent": cotangent, "segments": segments, "adapter_id": adapter_id, "input_weight": input_weight, "output_weight": output_weight, "norm_gain": norm_gain, "norm_shift": norm_shift, "attention_down": attention_down, "attention_up": attention_up, "expand_weight": expand_weight, "reduce_weight": reduce_weight, "expand_down": expand_down, "expand_up": expand_up, "reduce_down": reduce_down, "reduce_up": reduce_up}


@jax.custom_vjp
def low(v):
    return lax.optimization_barrier(v.astype(jnp.bfloat16)).astype(jnp.float32)

@jax.custom_vjp
def low_back(v):
    return v

def low_keep(v):
    return (low(v), None)

def low_pass(kept, grad):
    return (grad,)

def back_keep(v):
    return (v, None)

def back_low(kept, grad):
    return (low(grad),)
low.defvjp(low_keep, low_pass)
low_back.defvjp(back_keep, back_low)
epsilon = 1e-12
highest = lax.Precision.HIGHEST

def contract(form, left, right):
    return jnp.einsum(form, left, right, precision=highest)

def layer_norm(values, gains, shifts):
    average = lax.optimization_barrier(jnp.mean(values, axis=-1, keepdims=True))
    centered = values - average
    spread = lax.optimization_barrier(jnp.mean(centered * centered, axis=-1, keepdims=True))
    return centered * lax.rsqrt(spread + epsilon) * gains + shifts

def adapted(rows, chosen, weight, down_table, up_table):
    picked_down = contract('sa,axr->sxr', chosen, down_table)
    picked_up = contract('sa,are->sre', chosen, up_table)
    inner_rows = low_back(low(contract('slx,sxr->slr', rows, picked_down)))
    return contract('slx,xe->sle', rows, weight) + contract('slr,sre->sle', inner_rows, picked_up)

def attention(queries, key_rows, value_rows, segment):
    count, length = (queries.shape[0], queries.shape[1])
    queries = queries.reshape(count, length, HEADS, HEAD_DIM)
    key_rows = key_rows.reshape(count, length, HEADS, HEAD_DIM)
    value_rows = value_rows.reshape(count, length, HEADS, HEAD_DIM)
    scores = low_back(contract('sqhd,skhd->shqk', queries, key_rows) * HEAD_DIM ** (-0.5))
    same_doc = (segment[:, :, None] == segment[:, None, :])[:, None, :, :]
    masked = jnp.where(same_doc, scores, -1000000000.0)
    log_total = jax.scipy.special.logsumexp(masked, axis=-1, keepdims=True)
    weights = low(jnp.exp(masked - log_total))
    context = contract('shqk,skhd->sqhd', weights, value_rows)
    return context.reshape(count, length, HEADS * HEAD_DIM)

def forward(tokens, chosen, segment, frozen, attention_down, attention_up, expand_down, expand_up, reduce_down, reduce_up):
    input_weight, output_weight, norm_gain, norm_shift, expand_weight, reduce_weight = frozen
    projected = []
    for index in range(3):
        result = adapted(tokens, chosen, input_weight[index], attention_down[index], attention_up[index])
        projected.append(low_back(low(result)))
    context = low_back(low(attention(projected[0], projected[1], projected[2], segment)))
    branch = adapted(context, chosen, output_weight, attention_down[3], attention_up[3])
    hidden_one = tokens + low_back(branch)
    normed = layer_norm(hidden_one, norm_gain[0], norm_shift[0])
    normed_low = low(normed)
    expanded = low_back(adapted(normed_low, chosen, expand_weight, expand_down, expand_up))
    active = low(jax.nn.gelu(expanded, approximate=False))
    reduced = adapted(active, chosen, reduce_weight, reduce_down, reduce_up)
    hidden_two = normed + low_back(reduced)
    return layer_norm(hidden_two, norm_gain[1], norm_shift[1])

def reference(tokens, cotangent, segments, adapter_id, input_weight, output_weight, norm_gain, norm_shift, attention_down, attention_up, expand_weight, reduce_weight, expand_down, expand_up, reduce_down, reduce_up):
    group_size = math.gcd(SEQS, max(1, 4096 // SEQ_LEN))
    rounds = SEQS // group_size
    frozen = tuple((table.astype(jnp.float32) for table in (input_weight, output_weight, norm_gain, norm_shift, expand_weight, reduce_weight)))
    tables = tuple((table.astype(jnp.float32) for table in (attention_down, attention_up, expand_down, expand_up, reduce_down, reduce_up)))
    chosen_all = (adapter_id[:, None] == jnp.arange(ADAPT, dtype=jnp.int32)[None, :]).astype(jnp.float32)

    def one_round(carried, pieces):
        token_rows, cotangent_rows, segment_rows, chosen = pieces

        def forward_rows(token_values, *table_values):
            return forward(token_values, chosen, segment_rows, frozen, *table_values)
        output_rows, backward = jax.vjp(forward_rows, token_rows.astype(jnp.float32), *tables)
        gradients = backward(cotangent_rows.astype(jnp.float32))
        carried = tuple((summed + addend for summed, addend in zip(carried, gradients[1:])))
        return (carried, (output_rows.astype(jnp.bfloat16), gradients[0]))
    initial = tuple((jnp.zeros_like(table) for table in tables))
    pieces = (tokens.reshape(rounds, group_size, SEQ_LEN, D), cotangent.reshape(rounds, group_size, SEQ_LEN, D), segments.reshape(rounds, group_size, SEQ_LEN), chosen_all.reshape(rounds, group_size, ADAPT))
    totals, stacked = lax.scan(one_round, initial, pieces)
    outputs = stacked[0].reshape(SEQS, SEQ_LEN, D)
    token_grads = stacked[1].reshape(SEQS, SEQ_LEN, D)
    return (outputs, token_grads, totals[0], totals[1], totals[2], totals[3], totals[4], totals[5])
```

```python
import jax
import jax.numpy as jnp
from jax import lax
from jax.sharding import PartitionSpec as P

HEAD_DIM = 64
epsilon = 1e-12
low = jnp.bfloat16


def product(form, left, right):
    return jnp.einsum(form, left, right, preferred_element_type=jnp.float32)


def layer_norm(values, gains, shifts):
    average = jnp.mean(values, axis=-1, keepdims=True)
    centered = values - average
    spread = jnp.mean(centered * centered, axis=-1, keepdims=True)
    return centered * lax.rsqrt(spread + epsilon) * gains + shifts


def exact_gelu(values):
    return jax.nn.gelu(values, approximate=False)


def masked_scores(queries, key_rows, segment):
    scores = product("qhd,khd->hqk", queries, key_rows) * HEAD_DIM ** (-0.5)
    same_doc = segment[:, None] == segment[None, :]
    return jnp.where(same_doc[None], scores, -1000000000.0)


def heads(rows):
    return rows.reshape(rows.shape[0], -1, HEAD_DIM)


def attend_forward(queries, key_rows, value_rows, segment):
    masked = masked_scores(heads(queries), heads(key_rows), segment)
    largest = jnp.max(masked, axis=-1, keepdims=True)
    log_total = largest + jnp.log(jnp.sum(jnp.exp(masked - largest), axis=-1, keepdims=True))
    weights = jnp.exp(masked - log_total).astype(low)
    context = product("hqk,khd->qhd", weights, heads(value_rows))
    return context.reshape(queries.shape).astype(low), log_total


def attend_backward(queries, key_rows, value_rows, segment, log_total, context_back):
    scaling = HEAD_DIM ** (-0.5)
    masked = masked_scores(heads(queries), heads(key_rows), segment)
    weights = jnp.exp(masked - log_total)
    weights_back = product("qhd,khd->hqk", heads(context_back), heads(value_rows))
    row_dots = jnp.sum(weights * weights_back, axis=-1, keepdims=True)
    scores_back = (weights * (weights_back - row_dots)).astype(low)
    query_back = product("hqk,khd->qhd", scores_back, heads(key_rows)) * scaling
    key_back = product("hqk,qhd->khd", scores_back, heads(queries)) * scaling
    value_back = product("hqk,qhd->khd", weights.astype(low), heads(context_back))
    return tuple(g.reshape(queries.shape).astype(low) for g in (query_back, key_back, value_back))


def on_device(
    tokens,
    cotangent,
    segments,
    adapter_id,
    input_weight,
    output_weight,
    norm_gain,
    norm_shift,
    attention_down,
    attention_up,
    expand_weight,
    reduce_weight,
    expand_down,
    expand_up,
    reduce_down,
    reduce_up,
):
    devices = lax.axis_size("fsdp")
    tables, adapters, part, rank = attention_down.shape
    width = part * devices
    inner_width = reduce_weight.shape[0] * devices
    part_inner = reduce_weight.shape[0]
    lanes = adapters * rank
    x = tokens[0]
    length = x.shape[0]

    packed_attention = jnp.concatenate(
        [
            input_weight.transpose(1, 0, 2).reshape(part, 3 * width),
            output_weight,
            attention_down.transpose(2, 0, 1, 3).reshape(part, tables * lanes),
            attention_up.transpose(3, 0, 1, 2).reshape(part, tables * lanes),
            jnp.pad(
                jnp.concatenate([norm_gain, norm_shift], axis=0).T, ((0, 0), (0, lanes - 4))
            ),
        ],
        axis=1,
    )
    packed_expand = jnp.concatenate(
        [
            expand_weight,
            expand_down.transpose(1, 0, 2).reshape(part, lanes),
            reduce_up.transpose(2, 0, 1).reshape(part, lanes),
        ],
        axis=1,
    )
    packed_reduce = jnp.concatenate(
        [
            reduce_weight,
            reduce_down.transpose(1, 0, 2).reshape(part_inner, lanes),
            expand_up.transpose(2, 0, 1).reshape(part_inner, lanes),
        ],
        axis=1,
    )
    whole = lax.all_gather(packed_attention, "fsdp", axis=0, tiled=True)
    whole_expand = lax.all_gather(packed_expand, "fsdp", axis=0, tiled=True)
    whole_reduce = lax.all_gather(packed_reduce, "fsdp", axis=0, tiled=True)

    row = lax.broadcasted_iota(jnp.int32, (lanes, lanes), 0)
    col = lax.broadcasted_iota(jnp.int32, (lanes, lanes), 1)

    def picked(table, slot):
        choose = (
            (row // rank == adapter_id[0]) & (row % rank == col % rank) & (col // rank == slot)
        ).astype(low)
        return product("xa,ab->xb", table, choose).astype(low)

    off = 4 * width
    down = [
        picked(whole[:, off + t * lanes : off + (t + 1) * lanes], t) for t in range(tables)
    ]
    off = off + tables * lanes
    up = [picked(whole[:, off + t * lanes : off + (t + 1) * lanes], t) for t in range(tables)]
    off = off + tables * lanes
    norms = whole[:, off : off + 4].astype(jnp.float32).T
    gain_one, gain_two, shift_one, shift_two = norms[0], norms[1], norms[2], norms[3]
    down_in = down[0] + down[1] + down[2]
    w_in = [whole[:, t * width : (t + 1) * width] for t in range(3)]
    w_out = whole[:, 3 * width : 4 * width]

    inner_in = product("lx,xr->lr", x, down_in).astype(low)
    q, k, v = [
        (product("lx,xe->le", x, w_in[t]) + product("lr,er->le", inner_in, up[t])).astype(low)
        for t in range(3)
    ]
    segment = segments[0]
    context, log_total = attend_forward(q, k, v, segment)
    inner_out = product("lx,xr->lr", context, down[3]).astype(low)
    branch = product("lx,xe->le", context, w_out) + product("lr,er->le", inner_out, up[3])
    hidden_one = x.astype(jnp.float32) + branch
    normed, norm_one_back = jax.vjp(lambda h: layer_norm(h, gain_one, shift_one), hidden_one)
    normed_low = normed.astype(low)

    w_exp = whole_expand[:, :inner_width]
    w_red = whole_reduce[:, :width]
    exp_down = picked(whole_expand[:, inner_width : inner_width + lanes], 0)
    red_up = picked(whole_expand[:, inner_width + lanes :], 1)
    red_down = picked(whole_reduce[:, width : width + lanes], 1)
    exp_up = picked(whole_reduce[:, width + lanes :], 0)
    inner_exp = product("lx,xr->lr", normed_low, exp_down).astype(low)
    expanded = product("lx,xf->lf", normed_low, w_exp) + product("lr,fr->lf", inner_exp, exp_up)
    active, gelu_back = jax.vjp(exact_gelu, expanded)
    active_low = active.astype(low)
    inner_red = product("lf,fr->lr", active_low, red_down).astype(low)
    reduced = product("lf,fe->le", active_low, w_red) + product("lr,er->le", inner_red, red_up)
    hidden_two = normed + reduced
    output, norm_two_back = jax.vjp(lambda h: layer_norm(h, gain_two, shift_two), hidden_two)

    two_back = norm_two_back(cotangent[0].astype(jnp.float32))[0]
    reduced_back = two_back.astype(low)
    inner_red_back = product("le,er->lr", reduced_back, red_up).astype(low)
    active_back = product("le,fe->lf", reduced_back, w_red) + product(
        "lr,fr->lf", inner_red_back, red_down
    )
    expanded_back = gelu_back(active_back)[0].astype(low)
    inner_exp_back = product("lf,fr->lr", expanded_back, exp_up).astype(low)
    normed_back = (
        two_back
        + product("lf,xf->lx", expanded_back, w_exp)
        + product("lr,xr->lx", inner_exp_back, exp_down)
    )
    grad_feed = product("lx,lr->xr", normed_low, inner_exp_back) + product(
        "lx,lr->xr", reduced_back, inner_red
    )
    grad_inner = product("lf,lr->fr", expanded_back, inner_exp) + product(
        "lf,lr->fr", active_low, inner_red_back
    )

    one_back = norm_one_back(normed_back)[0]
    branch_back = one_back.astype(low)
    inner_out_back = product("le,er->lr", branch_back, up[3]).astype(low)
    context_back = (
        product("le,xe->lx", branch_back, w_out) + product("lr,xr->lx", inner_out_back, down[3])
    ).astype(low)
    backs = attend_backward(q, k, v, segment, log_total, context_back)
    inner_in_back = sum(product("le,er->lr", backs[t], up[t]) for t in range(3)).astype(low)
    tokens_back = (
        one_back
        + sum(product("le,xe->lx", backs[t], w_in[t]) for t in range(3))
        + product("lr,xr->lx", inner_in_back, down_in)
    )
    grad_down = product("lx,lr->xr", x, inner_in_back) + product(
        "lx,lr->xr", context, inner_out_back
    )

    def only(inner, slot):
        lane = lax.broadcasted_iota(jnp.int32, inner.shape, 1)
        return jnp.where(lane // rank == slot, inner, jnp.zeros_like(inner))

    grad_up = (
        sum(product("le,lr->er", backs[t], only(inner_in, t)) for t in range(3))
        + product("le,lr->er", branch_back, inner_out)
    )
    half = tables * rank
    chosen = (jnp.arange(adapters, dtype=jnp.int32) == adapter_id[0]).astype(low)
    fold = part_inner // part
    sent = jnp.concatenate(
        [
            grad_down[:, :half].reshape(devices, part, half),
            grad_up[:, :half].reshape(devices, part, half),
            grad_feed[:, : 2 * rank].reshape(devices, part, 2 * rank),
            grad_inner[:, : 2 * rank]
            .reshape(devices, fold, part, 2 * rank)
            .transpose(0, 2, 1, 3)
            .reshape(devices, part, fold * 2 * rank),
        ],
        axis=2,
    ).astype(low)
    sent = jnp.concatenate(
        [sent, jnp.broadcast_to(chosen, (devices, part, adapters))], axis=2
    )
    got = lax.all_to_all(sent, "fsdp", 0, 0, tiled=True)
    who = got[:, 0, -adapters:]
    total = product("sa,sxc->axc", who, got[:, :, :-adapters])
    down_grad = total[:, :, :half].reshape(adapters, part, tables, rank).transpose(2, 0, 1, 3)
    up_grad = total[:, :, half : 2 * half].reshape(adapters, part, tables, rank)
    up_grad = up_grad.transpose(2, 0, 3, 1)
    base = 2 * half
    expand_down_grad = total[:, :, base : base + rank]
    reduce_up_grad = total[:, :, base + rank : base + 2 * rank].transpose(0, 2, 1)
    inner_total = (
        total[:, :, base + 2 * rank :]
        .reshape(adapters, part, fold, 2 * rank)
        .transpose(0, 2, 1, 3)
        .reshape(adapters, part_inner, 2 * rank)
    )
    expand_up_grad = inner_total[:, :, :rank].transpose(0, 2, 1)
    reduce_down_grad = inner_total[:, :, rank:]
    return (
        output.astype(low)[None],
        tokens_back[None],
        down_grad,
        up_grad,
        expand_down_grad,
        expand_up_grad,
        reduce_down_grad,
        reduce_up_grad,
    )


def solution(mesh):
    placed = (
        P("fsdp", None, None),
        P("fsdp", None, None),
        P("fsdp", None),
        P("fsdp"),
        P(None, "fsdp", None),
        P("fsdp", None),
        P(None, "fsdp"),
        P(None, "fsdp"),
        P(None, None, "fsdp", None),
        P(None, None, None, "fsdp"),
        P("fsdp", None),
        P("fsdp", None),
        P(None, "fsdp", None),
        P(None, None, "fsdp"),
        P(None, "fsdp", None),
        P(None, None, "fsdp"),
    )
    return jax.shard_map(
        on_device,
        mesh=mesh,
        in_specs=placed,
        out_specs=(
            P("fsdp", None, None),
            P("fsdp", None, None),
            P(None, None, "fsdp", None),
            P(None, None, None, "fsdp"),
            P(None, "fsdp", None),
            P(None, None, "fsdp"),
            P(None, "fsdp", None),
            P(None, None, "fsdp"),
        ),
        check_vma=False,
    )
```

```python
import jax
import jax.numpy as jnp
from jax import lax
from jax.experimental import pallas as pl
from jax.experimental.pallas import tpu as pltpu
from jax.sharding import PartitionSpec as P

HEAD_DIM = 64
epsilon = 1e-12
low = jnp.bfloat16
wide = jnp.float32
scaling = HEAD_DIM ** (-0.5)
far = -1000000000.0


def nn(left, right):
    return lax.dot_general(left, right, (((1,), (0,)), ((), ())), preferred_element_type=wide)


def nt(left, right):
    return lax.dot_general(left, right, (((1,), (1,)), ((), ())), preferred_element_type=wide)


def tn(left, right):
    return lax.dot_general(left, right, (((0,), (0,)), ((), ())), preferred_element_type=wide)


def lane_of(values):
    return lax.broadcasted_iota(jnp.int32, values.shape, 1)


def only(values, first, last):
    lane = lane_of(values)
    return jnp.where((lane >= first) & (lane < last), values, jnp.zeros_like(values))


def normalize(values):
    average = jnp.mean(values, axis=-1, keepdims=True)
    centered = values - average
    spread = jnp.mean(centered * centered, axis=-1, keepdims=True)
    scale = lax.rsqrt(spread + epsilon)
    return centered * scale, scale


def normalize_back(grads, normal, scale):
    return scale * (
        grads
        - jnp.mean(grads, axis=-1, keepdims=True)
        - normal * jnp.mean(grads * normal, axis=-1, keepdims=True)
    )


def tile_of(width):
    return min(256, width)


def attend_kernel(
    rank,
    x_ref,
    seg_row_ref,
    seg_col_ref,
    sel_ref,
    whole_ref,
    q_ref,
    k_ref,
    v_ref,
    context_ref,
    lse_ref,
    inner_ref,
    tab_ref,
    hidden_ref,
    w_ref,
    raw_ref,
    mask_ref,
    stat_ref,
    sems,
):
    length, width = x_ref.shape
    lanes = inner_ref.shape[1]
    raw_width = raw_ref.shape[1]
    half = raw_width // 2

    def fetch(t):
        if t == 4:
            return pltpu.make_async_copy(
                whole_ref.at[:, pl.ds(4 * width, raw_width)], raw_ref, sems.at[t]
            )
        return pltpu.make_async_copy(
            whole_ref.at[:, pl.ds(t * width, width)], w_ref.at[t], sems.at[t]
        )

    for t in (4, 0, 1, 2, 3):
        fetch(t).start()
    mask_ref[...] = (seg_col_ref[...] == seg_row_ref[...]).astype(wide)
    fetch(4).wait()
    tab_ref[:, :lanes] = nn(raw_ref[:, :half], sel_ref[...]).astype(low)
    tab_ref[:, lanes:] = nn(raw_ref[:, half:], sel_ref[...]).astype(low)
    inner_in = only(nn(x_ref[...], tab_ref[:, :lanes]).astype(low), 0, 3 * rank)
    tile = tile_of(width)
    for t, out in enumerate((q_ref, k_ref, v_ref)):
        fetch(t).wait()
        inner_t = only(inner_in, t * rank, (t + 1) * rank)

        @pl.loop(0, width // tile)
        def _(j, t=t, out=out, inner_t=inner_t):
            cols = pl.ds(pl.multiple_of(j * tile, tile), tile)
            out[:, cols] = (
                nn(x_ref[...], w_ref[t, :, cols]) + nt(inner_t, tab_ref[cols, lanes:])
            ).astype(low)

    pair = 2 * HEAD_DIM
    rows_at_once = min(256, length)
    stat_ref[...] = jnp.zeros_like(stat_ref)

    @pl.loop(0, width // pair)
    def _(p):
        cols = pl.ds(pl.multiple_of(p * pair, pair), pair)
        for r in range(0, length, rows_at_once):
            rows = pl.ds(r, rows_at_once)
            left = lax.broadcasted_iota(jnp.int32, (rows_at_once, pair), 1) < HEAD_DIM
            query = q_ref[rows, cols]
            both = []
            for h in range(2):
                mine = left if h == 0 else jnp.logical_not(left)
                scores = nt(jnp.where(mine, query, jnp.zeros_like(query)), k_ref[:, cols])
                masked = jnp.where(mask_ref[rows, :] > 0.5, scores * scaling, far)
                largest = jnp.max(masked, axis=-1, keepdims=True)
                grown = jnp.exp(masked - largest)
                total = jnp.sum(grown, axis=-1, keepdims=True)
                weights = (grown * (1.0 / total)).astype(low)
                both.append(nn(weights, v_ref[:, cols]))
                lane = lax.broadcasted_iota(jnp.int32, (rows_at_once, stat_ref.shape[1]), 1)
                stat_ref[rows, :] = jnp.where(
                    lane == 2 * p + h, largest + jnp.log(total), stat_ref[rows, :]
                )
            context_ref[rows, cols] = jnp.where(left, both[0], both[1]).astype(low)

    lse_ref[...] = stat_ref[...].T
    inner_out = only(
        nn(context_ref[...], tab_ref[:, :lanes]).astype(low), 3 * rank, 4 * rank
    )
    inner_ref[...] = inner_in + inner_out
    fetch(3).wait()

    @pl.loop(0, width // tile)
    def _(j):
        cols = pl.ds(pl.multiple_of(j * tile, tile), tile)
        hidden_ref[:, cols] = x_ref[:, cols].astype(wide) + (
            nn(context_ref[...], w_ref[3, :, cols]) + nt(inner_out, tab_ref[cols, lanes:])
        )


def feed_kernel(
    rank,
    hidden_ref,
    cot_ref,
    norms_ref,
    sel_exp_ref,
    sel_red_ref,
    exp_ref,
    red_ref,
    output_ref,
    back_ref,
    grad_w_ref,
    grad_f_ref,
    we_ref,
    wr_ref,
    raw_w_ref,
    raw_f_ref,
    tab_w_ref,
    tab_f_ref,
    low_ref,
    active_ref,
    slope_ref,
    sum_ref,
    two_ref,
    sems,
    sems_r,
    sems_f,
):
    length, width = hidden_ref.shape
    chunks, _, chunk = we_ref.shape
    inner_width = chunks * chunk
    lanes = tab_w_ref.shape[1]

    def fetch_e(j):
        return pltpu.make_async_copy(
            exp_ref.at[:, pl.ds(pl.multiple_of(j * chunk, chunk), chunk)], we_ref.at[j], sems.at[j]
        )

    def fetch_r(j):
        return pltpu.make_async_copy(
            red_ref.at[pl.ds(pl.multiple_of(j * chunk, chunk), chunk), pl.ds(0, width)],
            wr_ref.at[j],
            sems_r.at[j],
        )

    def fetch_f(j):
        return pltpu.make_async_copy(
            red_ref.at[
                pl.ds(pl.multiple_of(j * chunk, chunk), chunk), pl.ds(width, 2 * lanes)
            ],
            raw_f_ref.at[j],
            sems_f.at[j],
        )

    raw_copy = pltpu.make_async_copy(
        exp_ref.at[:, pl.ds(inner_width, 2 * lanes)], raw_w_ref, sems.at[chunks]
    )
    raw_copy.start()

    @pl.loop(0, chunks)
    def _(j):
        fetch_e(j).start()
        fetch_f(j).start()
        fetch_r(j).start()

    normal, _ = normalize(hidden_ref[...])
    normed = normal * norms_ref[0:1, :] + norms_ref[2:3, :]
    low_ref[...] = normed.astype(low)
    sum_ref[...] = normed
    raw_copy.wait()
    tab_w_ref[...] = nn(raw_w_ref[...], sel_exp_ref[...]).astype(low)
    inner_exp = only(nn(low_ref[...], tab_w_ref[...]).astype(low), 0, rank)

    def forward(j, inner_sum):
        fetch_f(j).wait()
        tab_f_ref[j] = nn(raw_f_ref[j], sel_red_ref[...]).astype(low)
        fetch_e(j).wait()
        expanded = nn(low_ref[...], we_ref[j]) + nt(inner_exp, tab_f_ref[j])
        share = 0.5 * (1.0 + lax.erf(expanded * (2.0 ** -0.5)))
        density = jnp.exp(-0.5 * expanded * expanded) * 0.3989422804014327
        slope_ref[j] = share + expanded * density
        active = (expanded * share).astype(low)
        active_ref[j] = active
        fetch_r(j).wait()
        sum_ref[...] += nn(active, wr_ref[j])
        return inner_sum + nn(active, tab_f_ref[j])

    inner_sum = lax.fori_loop(0, chunks, forward, jnp.zeros((length, lanes), wide))
    inner_red = only(inner_sum.astype(low), rank, 2 * rank)
    normal, scale = normalize(sum_ref[...] + nt(inner_red, tab_w_ref[...]))
    output_ref[...] = (normal * norms_ref[1:2, :] + norms_ref[3:4, :]).astype(low)
    two_back = normalize_back(cot_ref[...].astype(wide) * norms_ref[1:2, :], normal, scale)
    reduced_back = two_back.astype(low)
    two_ref[...] = reduced_back
    inner_red_back = only(nn(reduced_back, tab_w_ref[...]).astype(low), rank, 2 * rank)
    sum_ref[...] = two_back

    def backward(j, inner_sum):
        active_back = nt(two_ref[...], wr_ref[j]) + nt(inner_red_back, tab_f_ref[j])
        expanded_back = (active_back * slope_ref[j]).astype(low)
        sum_ref[...] += nt(expanded_back, we_ref[j])
        cols = pl.ds(pl.multiple_of(j * chunk, chunk), chunk)
        grad_f_ref[:, cols] = (
            tn(inner_exp, expanded_back) + tn(inner_red_back, active_ref[j])
        )[: 2 * rank].astype(low)
        return inner_sum + nn(expanded_back, tab_f_ref[j])

    inner_sum = lax.fori_loop(0, chunks, backward, jnp.zeros((length, lanes), wide))
    inner_exp_back = only(inner_sum.astype(low), 0, rank)
    grad_w_ref[...] = (
        (tn(inner_exp_back, low_ref[...]) + tn(inner_red, two_ref[...])).T.astype(low)
    )
    normal, scale = normalize(hidden_ref[...])
    normed_back = sum_ref[...] + nt(inner_exp_back, tab_w_ref[...])
    back_ref[...] = normalize_back(normed_back * norms_ref[0:1, :], normal, scale)


def attend_back_kernel(
    rank,
    x_ref,
    seg_row_ref,
    seg_col_ref,
    q_ref,
    k_ref,
    v_ref,
    context_ref,
    lse_ref,
    inner_ref,
    tab_ref,
    one_ref,
    whole_ref,
    out_ref,
    grad_ref,
    w_ref,
    mask_ref,
    low_ref,
    cback_ref,
    dq_ref,
    dk_ref,
    dv_ref,
    gt_ref,
    sems,
):
    length, width = x_ref.shape
    lanes = inner_ref.shape[1]

    def fetch(t):
        return pltpu.make_async_copy(
            whole_ref.at[:, pl.ds(t * width, width)], w_ref.at[t], sems.at[t]
        )

    for t in (3, 0, 1, 2):
        fetch(t).start()
    mask_ref[...] = (seg_col_ref[...] == seg_row_ref[...]).astype(wide)
    low_ref[...] = one_ref[...].astype(low)
    inner_out_back = only(
        nn(low_ref[...], tab_ref[:, lanes:]).astype(low), 3 * rank, 4 * rank
    )
    tile = tile_of(width)
    fetch(3).wait()

    @pl.loop(0, width // tile)
    def _(j):
        cols = pl.ds(pl.multiple_of(j * tile, tile), tile)
        cback_ref[:, cols] = (
            nt(low_ref[...], w_ref[3, cols, :]) + nt(inner_out_back, tab_ref[cols, :lanes])
        ).astype(low)

    pair = 2 * HEAD_DIM

    @pl.loop(0, width // pair)
    def _(p):
        cols = pl.ds(pl.multiple_of(p * pair, pair), pair)
        left = lax.broadcasted_iota(jnp.int32, (length, pair), 1) < HEAD_DIM
        query, key, value = q_ref[:, cols], k_ref[:, cols], v_ref[:, cols]
        given = cback_ref[:, cols]
        made = []
        for h in range(2):
            mine = left if h == 0 else jnp.logical_not(left)
            zero = jnp.zeros_like(query)
            same = mask_ref[...] > 0.5
            scores = nt(key, jnp.where(mine, query, zero))
            log_total = lse_ref[pl.ds(2 * p + h, 1), :]
            weights = jnp.exp(jnp.where(same, scores * scaling, far) - log_total)
            weights_back = nt(value, jnp.where(mine, given, zero))
            dots = jnp.sum(weights * weights_back, axis=0, keepdims=True)
            scores_back = jnp.where(same, weights * (weights_back - dots), 0.0).astype(low)
            made.append(
                (
                    tn(scores_back, key),
                    nn(scores_back, query),
                    nn(weights.astype(low), given),
                )
            )
        dq_ref[:, cols] = (jnp.where(left, made[0][0], made[1][0]) * scaling).astype(low)
        dk_ref[:, cols] = (jnp.where(left, made[0][1], made[1][1]) * scaling).astype(low)
        dv_ref[:, cols] = jnp.where(left, made[0][2], made[1][2]).astype(low)

    backs = (dq_ref, dk_ref, dv_ref)
    inner_back = jnp.zeros((length, lanes), low)
    for t in range(3):
        inner_back = inner_back + only(
            nn(backs[t][...], tab_ref[:, lanes:]).astype(low), t * rank, (t + 1) * rank
        )
    inner_out = only(inner_ref[...], 3 * rank, 4 * rank)
    for t in range(3):
        fetch(t).wait()
    half = 4 * rank

    @pl.loop(0, width // tile)
    def _(j):
        cols = pl.ds(pl.multiple_of(j * tile, tile), tile)
        total = one_ref[:, cols] + nt(inner_back, tab_ref[cols, :lanes])
        for t in range(3):
            total = total + nt(backs[t][...], w_ref[t, cols, :])
        out_ref[:, cols] = total
        gt_ref[:half, cols] = (tn(inner_back, x_ref[:, cols]) + tn(inner_out_back, context_ref[:, cols]))[:half]
        grow = tn(inner_out, low_ref[:, cols])
        for t in range(3):
            grow = grow + tn(only(inner_ref[...], t * rank, (t + 1) * rank), backs[t][:, cols])
        gt_ref[half:, cols] = grow[:half]

    grad_ref[...] = gt_ref[...].T.astype(low)


def on_device(
    tokens,
    cotangent,
    segments,
    adapter_id,
    input_weight,
    output_weight,
    norm_gain,
    norm_shift,
    attention_down,
    attention_up,
    expand_weight,
    reduce_weight,
    expand_down,
    expand_up,
    reduce_down,
    reduce_up,
):
    devices = lax.axis_size("fsdp")
    tables, adapters, part, rank = attention_down.shape
    width = part * devices
    part_inner = reduce_weight.shape[0]
    inner_width = part_inner * devices
    lanes = adapters * rank
    x = tokens[0]
    length = x.shape[0]
    vmem_limit = 58 * 1024 * 1024

    def call(kernel, name, outs, scratch, inputs, spaces):
        return pl.pallas_call(
            kernel,
            name=name,
            out_shape=tuple(jax.ShapeDtypeStruct(s, d) for s, d in outs),
            in_specs=[
                pl.BlockSpec(memory_space=pl.ANY if a else pltpu.VMEM) for a in spaces
            ],
            out_specs=tuple(pl.BlockSpec(memory_space=pltpu.VMEM) for _ in outs),
            scratch_shapes=scratch,
            compiler_params=pltpu.CompilerParams(vmem_limit_bytes=vmem_limit),
        )(*inputs)

    packed_attention = jnp.concatenate(
        [
            input_weight.transpose(1, 0, 2).reshape(part, 3 * width),
            output_weight,
            attention_down.transpose(2, 0, 1, 3).reshape(part, tables * lanes),
            attention_up.transpose(3, 0, 1, 2).reshape(part, tables * lanes),
            jnp.pad(
                jnp.concatenate([norm_gain, norm_shift], axis=0).T, ((0, 0), (0, lanes - 4))
            ),
        ],
        axis=1,
    )
    packed_expand = jnp.concatenate(
        [
            expand_weight,
            expand_down.transpose(1, 0, 2).reshape(part, lanes),
            reduce_up.transpose(2, 0, 1).reshape(part, lanes),
        ],
        axis=1,
    )
    packed_reduce = jnp.concatenate(
        [
            reduce_weight,
            reduce_down.transpose(1, 0, 2).reshape(part_inner, lanes),
            expand_up.transpose(2, 0, 1).reshape(part_inner, lanes),
        ],
        axis=1,
    )
    whole = lax.all_gather(packed_attention, "fsdp", axis=0, tiled=True)
    whole_expand = lax.all_gather(packed_expand, "fsdp", axis=0, tiled=True)
    whole_reduce = lax.all_gather(packed_reduce, "fsdp", axis=0, tiled=True)

    def selection(slots):
        row = lax.broadcasted_iota(jnp.int32, (len(slots) * lanes, lanes), 0)
        col = lax.broadcasted_iota(jnp.int32, (len(slots) * lanes, lanes), 1)
        slot = jnp.zeros_like(row)
        for t, s in enumerate(slots):
            slot = jnp.where(row // lanes == t, s, slot)
        return (
            ((row % lanes) // rank == adapter_id[0])
            & (row % rank == col % rank)
            & (col // rank == slot)
        ).astype(low)

    off = 4 * width + 2 * tables * lanes
    norms = whole[:, off : off + 4].astype(wide).T
    seg_row = segments
    seg_col = segments.reshape(length, 1)

    dense = (length, width)
    q, k, v, context, lse, inner, tab, hidden = call(
        lambda *refs: attend_kernel(rank, *refs),
        "attend",
        [
            (dense, low),
            (dense, low),
            (dense, low),
            (dense, low),
            ((lanes, length), wide),
            ((length, lanes), low),
            ((width, 2 * lanes), low),
            (dense, wide),
        ],
        [
            pltpu.VMEM((4, width, width), low),
            pltpu.VMEM((width, 2 * tables * lanes), low),
            pltpu.VMEM((length, length), wide),
            pltpu.VMEM((length, lanes), wide),
            pltpu.SemaphoreType.DMA((5,)),
        ],
        (x, seg_row, seg_col, selection(range(tables)), whole),
        (0, 0, 0, 0, 1),
    )
    chunk = min(512, inner_width)
    chunks = inner_width // chunk
    output, one_back, grad_w, grad_f = call(
        lambda *refs: feed_kernel(rank, *refs),
        "feed",
        [
            (dense, low),
            (dense, wide),
            ((width, lanes), low),
            ((2 * rank, inner_width), low),
        ],
        [
            pltpu.VMEM((chunks, width, chunk), low),
            pltpu.VMEM((chunks, chunk, width), low),
            pltpu.VMEM((width, 2 * lanes), low),
            pltpu.VMEM((chunks, chunk, 2 * lanes), low),
            pltpu.VMEM((width, lanes), low),
            pltpu.VMEM((chunks, chunk, lanes), low),
            pltpu.VMEM(dense, low),
            pltpu.VMEM((chunks, length, chunk), low),
            pltpu.VMEM((chunks, length, chunk), wide),
            pltpu.VMEM(dense, wide),
            pltpu.VMEM(dense, low),
            pltpu.SemaphoreType.DMA((chunks + 1,)),
            pltpu.SemaphoreType.DMA((chunks,)),
            pltpu.SemaphoreType.DMA((chunks,)),
        ],
        (
            hidden,
            cotangent[0],
            norms,
            selection((0, 1)),
            selection((1, 0)),
            whole_expand,
            whole_reduce,
        ),
        (0, 0, 0, 0, 0, 1, 1),
    )
    tokens_back, grad_att = call(
        lambda *refs: attend_back_kernel(rank, *refs),
        "attend_back",
        [(dense, wide), ((width, lanes), low)],
        [
            pltpu.VMEM((4, width, width), low),
            pltpu.VMEM((length, length), wide),
            pltpu.VMEM(dense, low),
            pltpu.VMEM(dense, low),
            pltpu.VMEM(dense, low),
            pltpu.VMEM(dense, low),
            pltpu.VMEM(dense, low),
            pltpu.VMEM((2 * tables * rank, width), wide),
            pltpu.SemaphoreType.DMA((4,)),
        ],
        (x, seg_row, seg_col, q, k, v, context, lse, inner, tab, one_back, whole),
        (0, 0, 0, 0, 0, 0, 0, 0, 0, 0, 0, 1),
    )

    half = tables * rank
    per_feed = grad_w.reshape(devices, part, lanes)
    folded = 2 * rank * part_inner // lanes
    per_inner = (
        grad_f.reshape(2 * rank, devices, part_inner)
        .transpose(1, 0, 2)
        .reshape(devices, folded, lanes)
    )
    chosen = (jnp.arange(lanes, dtype=jnp.int32) == adapter_id[0]).astype(low)
    sent = jnp.concatenate(
        [
            per_feed,
            per_inner,
            jnp.broadcast_to(chosen, (devices, 8, lanes)),
        ],
        axis=1,
    )
    got_feed = lax.all_to_all(sent, "fsdp", 0, 0, tiled=True)
    got_att = lax.all_to_all(grad_att.reshape(devices, part, lanes), "fsdp", 0, 0, tiled=True)
    who = got_feed[:, -1, :adapters]

    def summed(got):
        return jnp.einsum("sa,sxc->axc", who, got, preferred_element_type=wide)

    total_feed = summed(got_feed[:, :-8])
    total = summed(got_att)
    down_grad = total[:, :, :half].reshape(adapters, part, tables, rank).transpose(2, 0, 1, 3)
    up_grad = total[:, :, half:].reshape(adapters, part, tables, rank).transpose(2, 0, 3, 1)
    expand_down_grad = total_feed[:, :part, :rank]
    reduce_up_grad = total_feed[:, :part, rank : 2 * rank].transpose(0, 2, 1)
    inner_total = total_feed[:, part:].reshape(adapters, 2 * rank, part_inner)
    expand_up_grad = inner_total[:, :rank]
    reduce_down_grad = inner_total[:, rank:].transpose(0, 2, 1)
    return (
        output[None],
        tokens_back[None],
        down_grad,
        up_grad,
        expand_down_grad,
        expand_up_grad,
        reduce_down_grad,
        reduce_up_grad,
    )


def solution(mesh):
    placed = (
        P("fsdp", None, None),
        P("fsdp", None, None),
        P("fsdp", None),
        P("fsdp"),
        P(None, "fsdp", None),
        P("fsdp", None),
        P(None, "fsdp"),
        P(None, "fsdp"),
        P(None, None, "fsdp", None),
        P(None, None, None, "fsdp"),
        P("fsdp", None),
        P("fsdp", None),
        P(None, "fsdp", None),
        P(None, None, "fsdp"),
        P(None, "fsdp", None),
        P(None, None, "fsdp"),
    )
    return jax.shard_map(
        on_device,
        mesh=mesh,
        in_specs=placed,
        out_specs=(
            P("fsdp", None, None),
            P("fsdp", None, None),
            P(None, None, "fsdp", None),
            P(None, None, None, "fsdp"),
            P(None, "fsdp", None),
            P(None, None, "fsdp"),
            P(None, "fsdp", None),
            P(None, None, "fsdp"),
        ),
        check_vma=False,
    )
```

```python
import jax
import jax.numpy as jnp
from jax import lax
from jax.experimental import pallas as pl
from jax.experimental.pallas import tpu as pltpu
from jax.sharding import PartitionSpec as P

HEAD_DIM = 64
epsilon = 1e-12
low = jnp.bfloat16
wide = jnp.float32
scaling = HEAD_DIM ** (-0.5)
far = -1000000000.0


def nn(left, right):
    return lax.dot_general(left, right, (((1,), (0,)), ((), ())), preferred_element_type=wide)


def nt(left, right):
    return lax.dot_general(left, right, (((1,), (1,)), ((), ())), preferred_element_type=wide)


def tn(left, right):
    return lax.dot_general(left, right, (((0,), (0,)), ((), ())), preferred_element_type=wide)


def lane_of(values):
    return lax.broadcasted_iota(jnp.int32, values.shape, 1)


def only(values, first, last):
    lane = lane_of(values)
    return jnp.where((lane >= first) & (lane < last), values, jnp.zeros_like(values))


def normalize(values):
    average = jnp.mean(values, axis=-1, keepdims=True)
    centered = values - average
    spread = jnp.mean(centered * centered, axis=-1, keepdims=True)
    scale = lax.rsqrt(spread + epsilon)
    return centered * scale, scale


def normalize_back(grads, normal, scale):
    return scale * (
        grads
        - jnp.mean(grads, axis=-1, keepdims=True)
        - normal * jnp.mean(grads * normal, axis=-1, keepdims=True)
    )


def tile_of(width):
    return min(256, width)


def fetcher(pieces, masks, place_ref, w_ref, sems):
    rows = pieces[0].shape[1]
    places = [place_ref[0] ^ m if m is not None else 0 for ms in masks for m in ms]

    def start(first, size, sem):
        at = 0
        for piece, ms in zip(pieces, masks):
            for slot in range(len(ms)):
                pltpu.make_async_copy(
                    piece.at[slot, :, pl.ds(first, size)],
                    w_ref.at[pl.ds(pl.multiple_of(places[at] * rows, rows), rows), pl.ds(first, size)],
                    sems.at[sem],
                ).start()
                at += 1

    def wait(first, size, sem):
        span = w_ref.at[:, pl.ds(first, size)]
        pltpu.make_async_copy(span, span, sems.at[sem]).wait()

    return start, wait


def attend_kernel(
    rank,
    masks,
    place_ref,
    x_ref,
    seg_row_ref,
    seg_col_ref,
    sel_ref,
    *refs,
):
    pieces, refs = refs[: len(masks)], refs[len(masks) :]
    (
        q_ref,
        k_ref,
        v_ref,
        context_ref,
        lse_ref,
        inner_ref,
        tab_ref,
        norms_ref,
        hidden_ref,
        w_ref,
        mask_ref,
        stat_ref,
        sems,
    ) = refs
    length, width = x_ref.shape
    lanes = inner_ref.shape[1]
    half = sel_ref.shape[0]
    start, wait = fetcher(pieces, masks, place_ref, w_ref, sems)
    spans = (
        (4 * width, w_ref.shape[1] - 4 * width, 0),
        (0, 3 * width, 1),
        (3 * width, width, 2),
    )
    for span in spans:
        start(*span)
    mask_ref[...] = (seg_col_ref[...] == seg_row_ref[...]).astype(wide)
    wait(*spans[0])
    off = 4 * width
    tab_ref[:, :lanes] = nn(w_ref[:, off : off + half], sel_ref[...]).astype(low)
    tab_ref[:, lanes:] = nn(w_ref[:, off + half : off + 2 * half], sel_ref[...]).astype(low)
    norms_ref[...] = w_ref[:, off + 2 * half :].astype(wide).T[:8]
    inner_in = only(nn(x_ref[...], tab_ref[:, :lanes]).astype(low), 0, 3 * rank)
    tile = tile_of(width)
    wait(*spans[1])
    for t, out in enumerate((q_ref, k_ref, v_ref)):
        inner_t = only(inner_in, t * rank, (t + 1) * rank)

        @pl.loop(0, width // tile)
        def _(j, t=t, out=out, inner_t=inner_t):
            cols = pl.ds(pl.multiple_of(j * tile, tile), tile)
            out[:, cols] = (
                nn(x_ref[...], w_ref[:, pl.ds(pl.multiple_of(t * width + j * tile, tile), tile)])
                + nt(inner_t, tab_ref[cols, lanes:])
            ).astype(low)

    pair = 2 * HEAD_DIM
    rows_at_once = min(256, length)
    stat_ref[...] = jnp.zeros_like(stat_ref)

    @pl.loop(0, width // pair)
    def _(p):
        cols = pl.ds(pl.multiple_of(p * pair, pair), pair)
        for r in range(0, length, rows_at_once):
            rows = pl.ds(r, rows_at_once)
            left = lax.broadcasted_iota(jnp.int32, (rows_at_once, pair), 1) < HEAD_DIM
            query = q_ref[rows, cols]
            both = []
            for h in range(2):
                mine = left if h == 0 else jnp.logical_not(left)
                scores = nt(jnp.where(mine, query, jnp.zeros_like(query)), k_ref[:, cols])
                masked = jnp.where(mask_ref[rows, :] > 0.5, scores * scaling, far)
                largest = jnp.max(masked, axis=-1, keepdims=True)
                grown = jnp.exp(masked - largest)
                total = jnp.sum(grown, axis=-1, keepdims=True)
                weights = (grown * (1.0 / total)).astype(low)
                both.append(nn(weights, v_ref[:, cols]))
                lane = lax.broadcasted_iota(jnp.int32, (rows_at_once, stat_ref.shape[1]), 1)
                stat_ref[rows, :] = jnp.where(
                    lane == 2 * p + h, largest + jnp.log(total), stat_ref[rows, :]
                )
            context_ref[rows, cols] = jnp.where(left, both[0], both[1]).astype(low)

    lse_ref[...] = stat_ref[...].T
    inner_out = only(
        nn(context_ref[...], tab_ref[:, :lanes]).astype(low), 3 * rank, 4 * rank
    )
    inner_ref[...] = inner_in + inner_out
    wait(*spans[2])

    @pl.loop(0, width // tile)
    def _(j):
        cols = pl.ds(pl.multiple_of(j * tile, tile), tile)
        hidden_ref[:, cols] = x_ref[:, cols].astype(wide) + (
            nn(context_ref[...], w_ref[:, pl.ds(pl.multiple_of(3 * width + j * tile, tile), tile)])
            + nt(inner_out, tab_ref[cols, lanes:])
        )


def feed_kernel(
    rank,
    fold,
    hidden_ref,
    cot_ref,
    norms_ref,
    sel_exp_ref,
    sel_red_ref,
    exp_ref,
    red_ref,
    output_ref,
    back_ref,
    grad_w_ref,
    grad_f_ref,
    we_ref,
    wr_ref,
    raw_w_ref,
    raw_f_ref,
    tab_w_ref,
    tab_f_ref,
    low_ref,
    active_ref,
    slope_ref,
    sum_ref,
    two_ref,
    sems,
    sems_r,
    sems_f,
):
    length, width = hidden_ref.shape
    chunks, _, chunk = we_ref.shape
    inner_width = chunks * chunk
    lanes = tab_w_ref.shape[1]

    def fetch_e(j):
        return pltpu.make_async_copy(
            exp_ref.at[:, pl.ds(pl.multiple_of(j * chunk, chunk), chunk)], we_ref.at[j], sems.at[j]
        )

    owners = chunk // (fold * wr_ref.shape[-2]) if fold else 0
    red_width = width + 2 * lanes

    def fetch_rows(j, first, size, into, sem):
        if not fold:
            return [
                pltpu.make_async_copy(
                    red_ref.at[pl.ds(pl.multiple_of(j * chunk, chunk), chunk), pl.ds(first, size)],
                    into.at[j],
                    sem.at[j, 0],
                )
            ]
        return [
            pltpu.make_async_copy(
                red_ref.at[
                    pl.ds(j * owners, owners),
                    :,
                    pl.ds(inner_width + 2 * lanes + d * red_width + first, size),
                ],
                into.at[j, :, d],
                sem.at[j, d],
            )
            for d in range(fold)
        ]

    def fetch_r(j):
        return fetch_rows(j, 0, width, wr_ref, sems_r)

    def fetch_f(j):
        return fetch_rows(j, width, 2 * lanes, raw_f_ref, sems_f)

    def rows_of(ref, j):
        return ref[j].reshape(chunk, ref.shape[-1])

    raw_copy = pltpu.make_async_copy(
        exp_ref.at[:, pl.ds(inner_width, 2 * lanes)], raw_w_ref, sems.at[chunks]
    )
    raw_copy.start()

    @pl.loop(0, chunks)
    def _(j):
        fetch_e(j).start()
        for copy in fetch_f(j) + fetch_r(j):
            copy.start()

    normal, _ = normalize(hidden_ref[...])
    normed = normal * norms_ref[0:1, :] + norms_ref[2:3, :]
    low_ref[...] = normed.astype(low)
    sum_ref[...] = normed
    raw_copy.wait()
    tab_w_ref[...] = nn(raw_w_ref[...], sel_exp_ref[...]).astype(low)
    inner_exp = only(nn(low_ref[...], tab_w_ref[...]).astype(low), 0, rank)

    def forward(j, inner_sum):
        for copy in fetch_f(j):
            copy.wait()
        tab_f_ref[j] = nn(rows_of(raw_f_ref, j), sel_red_ref[...]).astype(low)
        fetch_e(j).wait()
        expanded = nn(low_ref[...], we_ref[j]) + nt(inner_exp, tab_f_ref[j])
        share = 0.5 * (1.0 + lax.erf(expanded * (2.0 ** -0.5)))
        density = jnp.exp(-0.5 * expanded * expanded) * 0.3989422804014327
        slope_ref[j] = share + expanded * density
        active = (expanded * share).astype(low)
        active_ref[j] = active
        for copy in fetch_r(j):
            copy.wait()
        sum_ref[...] += nn(active, rows_of(wr_ref, j))
        return inner_sum + nn(active, tab_f_ref[j])

    inner_sum = lax.fori_loop(0, chunks, forward, jnp.zeros((length, lanes), wide))
    inner_red = only(inner_sum.astype(low), rank, 2 * rank)
    normal, scale = normalize(sum_ref[...] + nt(inner_red, tab_w_ref[...]))
    output_ref[...] = (normal * norms_ref[1:2, :] + norms_ref[3:4, :]).astype(low)
    two_back = normalize_back(cot_ref[...].astype(wide) * norms_ref[1:2, :], normal, scale)
    reduced_back = two_back.astype(low)
    two_ref[...] = reduced_back
    inner_red_back = only(nn(reduced_back, tab_w_ref[...]).astype(low), rank, 2 * rank)
    sum_ref[...] = two_back

    def backward(j, inner_sum):
        active_back = nt(two_ref[...], rows_of(wr_ref, j)) + nt(inner_red_back, tab_f_ref[j])
        expanded_back = (active_back * slope_ref[j]).astype(low)
        sum_ref[...] += nt(expanded_back, we_ref[j])
        cols = pl.ds(pl.multiple_of(j * chunk, chunk), chunk)
        grad_f_ref[:, cols] = (
            tn(inner_exp, expanded_back) + tn(inner_red_back, active_ref[j])
        )[: 2 * rank].astype(low)
        return inner_sum + nn(expanded_back, tab_f_ref[j])

    inner_sum = lax.fori_loop(0, chunks, backward, jnp.zeros((length, lanes), wide))
    inner_exp_back = only(inner_sum.astype(low), 0, rank)
    grad_w_ref[...] = (
        (tn(inner_exp_back, low_ref[...]) + tn(inner_red, two_ref[...])).T.astype(low)
    )
    normal, scale = normalize(hidden_ref[...])
    normed_back = sum_ref[...] + nt(inner_exp_back, tab_w_ref[...])
    back_ref[...] = normalize_back(normed_back * norms_ref[0:1, :], normal, scale)


def attend_back_kernel(
    rank,
    masks,
    place_ref,
    x_ref,
    seg_row_ref,
    seg_col_ref,
    q_ref,
    k_ref,
    v_ref,
    context_ref,
    lse_ref,
    inner_ref,
    tab_ref,
    one_ref,
    *refs,
):
    pieces, refs = refs[: len(masks)], refs[len(masks) :]
    (
        out_ref,
        grad_ref,
        w_ref,
        mask_ref,
        low_ref,
        cback_ref,
        dq_ref,
        dk_ref,
        dv_ref,
        gt_ref,
        sems,
    ) = refs
    length, width = x_ref.shape
    lanes = inner_ref.shape[1]
    start, wait = fetcher(pieces, masks, place_ref, w_ref, sems)
    spans = ((3 * width, width, 0), (0, 3 * width, 1))
    for span in spans:
        start(*span)
    mask_ref[...] = (seg_col_ref[...] == seg_row_ref[...]).astype(wide)
    low_ref[...] = one_ref[...].astype(low)
    inner_out_back = only(
        nn(low_ref[...], tab_ref[:, lanes:]).astype(low), 3 * rank, 4 * rank
    )
    tile = tile_of(width)
    wait(*spans[0])

    @pl.loop(0, width // tile)
    def _(j):
        cols = pl.ds(pl.multiple_of(j * tile, tile), tile)
        cback_ref[:, cols] = (
            nt(low_ref[...], w_ref[cols, 3 * width :]) + nt(inner_out_back, tab_ref[cols, :lanes])
        ).astype(low)

    pair = 2 * HEAD_DIM

    @pl.loop(0, width // pair)
    def _(p):
        cols = pl.ds(pl.multiple_of(p * pair, pair), pair)
        left = lax.broadcasted_iota(jnp.int32, (length, pair), 1) < HEAD_DIM
        query, key, value = q_ref[:, cols], k_ref[:, cols], v_ref[:, cols]
        given = cback_ref[:, cols]
        made = []
        for h in range(2):
            mine = left if h == 0 else jnp.logical_not(left)
            zero = jnp.zeros_like(query)
            same = mask_ref[...] > 0.5
            scores = nt(key, jnp.where(mine, query, zero))
            log_total = lse_ref[pl.ds(2 * p + h, 1), :]
            weights = jnp.exp(jnp.where(same, scores * scaling, far) - log_total)
            weights_back = nt(value, jnp.where(mine, given, zero))
            dots = jnp.sum(weights * weights_back, axis=0, keepdims=True)
            scores_back = jnp.where(same, weights * (weights_back - dots), 0.0).astype(low)
            made.append(
                (
                    tn(scores_back, key),
                    nn(scores_back, query),
                    nn(weights.astype(low), given),
                )
            )
        dq_ref[:, cols] = (jnp.where(left, made[0][0], made[1][0]) * scaling).astype(low)
        dk_ref[:, cols] = (jnp.where(left, made[0][1], made[1][1]) * scaling).astype(low)
        dv_ref[:, cols] = jnp.where(left, made[0][2], made[1][2]).astype(low)

    backs = (dq_ref, dk_ref, dv_ref)
    inner_back = jnp.zeros((length, lanes), low)
    for t in range(3):
        inner_back = inner_back + only(
            nn(backs[t][...], tab_ref[:, lanes:]).astype(low), t * rank, (t + 1) * rank
        )
    inner_out = only(inner_ref[...], 3 * rank, 4 * rank)
    wait(*spans[1])
    half = 4 * rank

    @pl.loop(0, width // tile)
    def _(j):
        cols = pl.ds(pl.multiple_of(j * tile, tile), tile)
        total = one_ref[:, cols] + nt(inner_back, tab_ref[cols, :lanes])
        for t in range(3):
            total = total + nt(backs[t][...], w_ref[cols, t * width : (t + 1) * width])
        out_ref[:, cols] = total
        gt_ref[:half, cols] = (tn(inner_back, x_ref[:, cols]) + tn(inner_out_back, context_ref[:, cols]))[:half]
        grow = tn(inner_out, low_ref[:, cols])
        for t in range(3):
            grow = grow + tn(only(inner_ref[...], t * rank, (t + 1) * rank), backs[t][:, cols])
        gt_ref[half:, cols] = grow[:half]

    grad_ref[...] = gt_ref[...].T.astype(low)


def on_device(
    tokens,
    cotangent,
    segments,
    adapter_id,
    input_weight,
    output_weight,
    norm_gain,
    norm_shift,
    attention_down,
    attention_up,
    expand_weight,
    reduce_weight,
    expand_down,
    expand_up,
    reduce_down,
    reduce_up,
):
    devices = lax.axis_size("fsdp")
    tables, adapters, part, rank = attention_down.shape
    width = part * devices
    part_inner = reduce_weight.shape[0]
    inner_width = part_inner * devices
    lanes = adapters * rank
    x = tokens[0]
    length = x.shape[0]
    vmem_limit = 58 * 1024 * 1024

    def call(kernel, name, outs, scratch, inputs, spaces):
        return pl.pallas_call(
            kernel,
            name=name,
            out_shape=tuple(jax.ShapeDtypeStruct(s, d) for s, d in outs),
            in_specs=[
                pl.BlockSpec(memory_space=(pltpu.VMEM, pl.ANY, pltpu.SMEM)[a]) for a in spaces
            ],
            out_specs=tuple(pl.BlockSpec(memory_space=pltpu.VMEM) for _ in outs),
            scratch_shapes=scratch,
            compiler_params=pltpu.CompilerParams(vmem_limit_bytes=vmem_limit),
        )(*inputs)

    packed_attention = jnp.concatenate(
        [
            input_weight.transpose(1, 0, 2).reshape(part, 3 * width),
            output_weight,
            attention_down.transpose(2, 0, 1, 3).reshape(part, tables * lanes),
            attention_up.transpose(3, 0, 1, 2).reshape(part, tables * lanes),
            jnp.pad(
                jnp.concatenate([norm_gain, norm_shift], axis=0).T, ((0, 0), (0, lanes - 4))
            ),
        ],
        axis=1,
    )
    packed_expand = jnp.concatenate(
        [
            expand_weight,
            expand_down.transpose(1, 0, 2).reshape(part, lanes),
            reduce_up.transpose(2, 0, 1).reshape(part, lanes),
        ],
        axis=1,
    )
    packed_reduce = jnp.concatenate(
        [
            reduce_weight,
            reduce_down.transpose(1, 0, 2).reshape(part_inner, lanes),
            expand_up.transpose(2, 0, 1).reshape(part_inner, lanes),
        ],
        axis=1,
    )
    place = lax.axis_index("fsdp")
    if devices == 32:
        fold = part_inner // part
        feed_packed = jnp.concatenate(
            [
                packed_expand,
                packed_reduce.reshape(fold, part, -1).transpose(1, 0, 2).reshape(part, -1),
            ],
            axis=1,
        )
        whole_feed = lax.all_gather(feed_packed, "fsdp", axis=0, tiled=True)
        feeds = (whole_feed, whole_feed.reshape(devices, part, -1))

        def swap(rows, bit):
            return lax.ppermute(rows, "fsdp", [(i, i ^ bit) for i in range(devices)])

        near = swap(packed_attention, 8)
        middle = swap(packed_attention, 16)
        distant = swap(packed_attention, 24)
        here_low = jnp.stack([packed_attention, near])
        here_high = jnp.stack([middle, distant])
        x_low, y_low = swap(here_low, 2), swap(here_low, 4)
        x_high, y_high = swap(here_high, 2), swap(here_high, 4)
        both_low, both_high = swap(x_low, 4), swap(y_high, 2)
        pieces, masks = [], []
        for piece, mask in (
            (here_low, 0),
            (here_high, 16),
            (x_low, 2),
            (y_low, 4),
            (x_high, 18),
            (y_high, 20),
            (both_low, 6),
            (both_high, 22),
        ):
            pieces += [piece, swap(piece, 1)]
            masks += [(mask, mask ^ 8), (mask ^ 1, mask ^ 9)]
    else:
        fold = 0
        pieces = [lax.all_gather(packed_attention, "fsdp", axis=0, tiled=True)[None]]
        masks = [(None,)]
        feeds = tuple(
            lax.all_gather(packed, "fsdp", axis=0, tiled=True)
            for packed in (packed_expand, packed_reduce)
        )

    def selection(slots):
        row = lax.broadcasted_iota(jnp.int32, (len(slots) * lanes, lanes), 0)
        col = lax.broadcasted_iota(jnp.int32, (len(slots) * lanes, lanes), 1)
        slot = jnp.zeros_like(row)
        for t, s in enumerate(slots):
            slot = jnp.where(row // lanes == t, s, slot)
        return (
            ((row % lanes) // rank == adapter_id[0])
            & (row % rank == col % rank)
            & (col // rank == slot)
        ).astype(low)

    seg_row = segments
    seg_col = segments.reshape(length, 1)

    dense = (length, width)
    q, k, v, context, lse, inner, tab, norms, hidden = call(
        lambda *refs: attend_kernel(rank, masks, *refs),
        "attend",
        [
            (dense, low),
            (dense, low),
            (dense, low),
            (dense, low),
            ((lanes, length), wide),
            ((length, lanes), low),
            ((width, 2 * lanes), low),
            ((8, width), wide),
            (dense, wide),
        ],
        [
            pltpu.VMEM((width, pieces[0].shape[2]), low),
            pltpu.VMEM((length, length), wide),
            pltpu.VMEM((length, lanes), wide),
            pltpu.SemaphoreType.DMA((3,)),
        ],
        (place[None], x, seg_row, seg_col, selection(range(tables)), *pieces),
        (2, 0, 0, 0, 0) + (1,) * len(pieces),
    )
    chunk = min(512, inner_width)
    chunks = inner_width // chunk
    rows_shape = (chunks, chunk // part_inner, fold, part) if fold else (chunks, chunk)
    output, one_back, grad_w, grad_f = call(
        lambda *refs: feed_kernel(rank, fold, *refs),
        "feed",
        [
            (dense, low),
            (dense, wide),
            ((width, lanes), low),
            ((2 * rank, inner_width), low),
        ],
        [
            pltpu.VMEM((chunks, width, chunk), low),
            pltpu.VMEM(rows_shape + (width,), low),
            pltpu.VMEM((width, 2 * lanes), low),
            pltpu.VMEM(rows_shape + (2 * lanes,), low),
            pltpu.VMEM((width, lanes), low),
            pltpu.VMEM((chunks, chunk, lanes), low),
            pltpu.VMEM(dense, low),
            pltpu.VMEM((chunks, length, chunk), low),
            pltpu.VMEM((chunks, length, chunk), wide),
            pltpu.VMEM(dense, wide),
            pltpu.VMEM(dense, low),
            pltpu.SemaphoreType.DMA((chunks + 1,)),
            pltpu.SemaphoreType.DMA((chunks, max(fold, 1))),
            pltpu.SemaphoreType.DMA((chunks, max(fold, 1))),
        ],
        (
            hidden,
            cotangent[0],
            norms,
            selection((0, 1)),
            selection((1, 0)),
            *feeds,
        ),
        (0, 0, 0, 0, 0, 1, 1),
    )
    tokens_back, grad_att = call(
        lambda *refs: attend_back_kernel(rank, masks, *refs),
        "attend_back",
        [(dense, wide), ((width, lanes), low)],
        [
            pltpu.VMEM((width, 4 * width), low),
            pltpu.VMEM((length, length), wide),
            pltpu.VMEM(dense, low),
            pltpu.VMEM(dense, low),
            pltpu.VMEM(dense, low),
            pltpu.VMEM(dense, low),
            pltpu.VMEM(dense, low),
            pltpu.VMEM((2 * tables * rank, width), wide),
            pltpu.SemaphoreType.DMA((2,)),
        ],
        (place[None], x, seg_row, seg_col, q, k, v, context, lse, inner, tab, one_back, *pieces),
        (2,) + (0,) * 11 + (1,) * len(pieces),
    )

    half = tables * rank
    per_feed = grad_w.reshape(devices, part, lanes)
    folded = 2 * rank * part_inner // lanes
    per_inner = (
        grad_f.reshape(2 * rank, devices, part_inner)
        .transpose(1, 0, 2)
        .reshape(devices, folded, lanes)
    )
    chosen = (jnp.arange(lanes, dtype=jnp.int32) == adapter_id[0]).astype(low)
    sent = jnp.concatenate(
        [
            per_feed,
            per_inner,
            jnp.broadcast_to(chosen, (devices, 8, lanes)),
        ],
        axis=1,
    )
    got_feed = lax.all_to_all(sent, "fsdp", 0, 0, tiled=True)
    got_att = lax.all_to_all(grad_att.reshape(devices, part, lanes), "fsdp", 0, 0, tiled=True)
    who = got_feed[:, -1, :adapters]

    def summed(got):
        return jnp.einsum("sa,sxc->axc", who, got, preferred_element_type=wide)

    total_feed = summed(got_feed[:, :-8])
    total = summed(got_att)
    down_grad = total[:, :, :half].reshape(adapters, part, tables, rank).transpose(2, 0, 1, 3)
    up_grad = total[:, :, half:].reshape(adapters, part, tables, rank).transpose(2, 0, 3, 1)
    expand_down_grad = total_feed[:, :part, :rank]
    reduce_up_grad = total_feed[:, :part, rank : 2 * rank].transpose(0, 2, 1)
    inner_total = total_feed[:, part:].reshape(adapters, 2 * rank, part_inner)
    expand_up_grad = inner_total[:, :rank]
    reduce_down_grad = inner_total[:, rank:].transpose(0, 2, 1)
    return (
        output[None],
        tokens_back[None],
        down_grad,
        up_grad,
        expand_down_grad,
        expand_up_grad,
        reduce_down_grad,
        reduce_up_grad,
    )


def solution(mesh):
    placed = (
        P("fsdp", None, None),
        P("fsdp", None, None),
        P("fsdp", None),
        P("fsdp"),
        P(None, "fsdp", None),
        P("fsdp", None),
        P(None, "fsdp"),
        P(None, "fsdp"),
        P(None, None, "fsdp", None),
        P(None, None, None, "fsdp"),
        P("fsdp", None),
        P("fsdp", None),
        P(None, "fsdp", None),
        P(None, None, "fsdp"),
        P(None, "fsdp", None),
        P(None, None, "fsdp"),
    )
    return jax.shard_map(
        on_device,
        mesh=mesh,
        in_specs=placed,
        out_specs=(
            P("fsdp", None, None),
            P("fsdp", None, None),
            P(None, None, "fsdp", None),
            P(None, None, None, "fsdp"),
            P(None, "fsdp", None),
            P(None, None, "fsdp"),
            P(None, "fsdp", None),
            P(None, None, "fsdp"),
        ),
        check_vma=False,
    )
```
